32 devices in a mesh: dp: 16 (over z, y, x), tensor: 2 (over core).
Axes of the slice: x: 2, y: 2, z: 4, core: 2. Of those that a mesh axis runs over, the one named last changes fastest.
Arguments:
- block_input: bfloat16 [2048, 1024], P('dp'), may hold values from -6 to 6
- document_ids: int32 [2048], P('dp'), may hold values from -1 to 127, as said below
- heads_weight: bfloat16 [2, 3, 1024, 1024], P(None, None, 'dp', 'tensor'), may hold values from -0.1875 to 0.1875
- merge_weight: bfloat16 [2, 1024, 1024], P(None, 'tensor', 'dp'), may hold values from -0.75 to 0.75
- up_weight: bfloat16 [2, 1024, 4096], P(None, 'dp', 'tensor'), may hold values from -0.1875 to 0.1875
- down_weight: bfloat16 [2, 4096, 1024], P(None, 'tensor', 'dp'), may hold values from -0.09375 to 0.09375
- query_value_bias: float32 [2, 2, 1024], P(None, None, 'tensor'), may hold values from -3 to 3
- up_bias: float32 [2, 4096], P(None, 'tensor'), may hold values from -3 to 3
- output_bias: float32 [2, 2, 1024], replicated, may hold values from -3 to 3
- norm_gain: float32 [2, 2, 1024], replicated, may hold values from 0.5 to 1.5
- norm_shift: float32 [2, 2, 1024], replicated, may hold values from -3 to 3
- cotangent: bfloat16 [2048, 1024], P('dp'), may hold values from -6 to 6
Outputs:
- block_output: bfloat16 [2048, 1024], P('dp')
- grad_input: float32 [2048, 1024], P('dp')
- grad_heads_weight: float32 [2, 3, 1024, 1024], P(None, None, 'dp', 'tensor')
- grad_merge_weight: float32 [2, 1024, 1024], P(None, 'tensor', 'dp')
- grad_up_weight: float32 [2, 1024, 4096], P(None, 'dp', 'tensor')
- grad_down_weight: float32 [2, 4096, 1024], P(None, 'tensor', 'dp')
- grad_query_value_bias: float32 [2, 2, 1024], P(None, None, 'tensor')
- grad_up_bias: float32 [2, 4096], P(None, 'tensor')
- grad_output_bias: float32 [2, 2, 1024], replicated
- grad_norm_gain: float32 [2, 2, 1024], replicated
- grad_norm_shift: float32 [2, 2, 1024], replicated
The draws below stay inside these ranges and needn't reach their ends.
Inputs may be any that keep to these rules, and one draw needn't show every extreme that they name: `document_ids`: in each block of 128 consecutive slots (the slots of one dp index) the live slots come first: runs of equal values, each the position within the block of its run's first slot, followed by -1 up to the block's end; at least a quarter of every block is live, at least one block has no padding and at least one has some.
All inputs are finite; a program needn't handle non-finite values.
Results may differ from the reference program's by a relative error of at most 0.018.
Values may be sent and summed in bfloat16 or wider, within the bound.
No kernel may reach another device: no remote copies, remote signals or barrier semaphores. Data moves between devices by JAX's collectives and lax.ppermute only.
A program may use at most 192 MiB of HBM per device.

```python
import jax
import jax.numpy as jnp
from jax import lax

D = 1024
HEAD_DIM = 64
FF = 4096
LAYERS = 2
TOK_DEV = 128
TOKENS = 2048


def draw_document_ids(key, part):
    devices = TOKENS // TOK_DEV
    key_fill, key_full, key_start = jax.random.split(key, 3)
    filled = jax.random.randint(key_fill, (devices,), TOK_DEV // 4, TOK_DEV)
    full_rank = jax.random.randint(key_full, (), 0, devices)
    device_rank = jnp.arange(devices)[:, None]
    filled = jnp.where(device_rank[:, 0] == full_rank, TOK_DEV, filled)
    position = jnp.arange(TOK_DEV)[None, :]
    starts = jax.random.randint(key_start, (devices, TOK_DEV), 0, max(TOK_DEV // 4, 2)) == 0
    starts = starts | (position == 0) | (device_rank == full_rank) & (position == TOK_DEV - 1)
    leading = lax.cummax(jnp.where(starts, position, 0), axis=1)
    doc_id = jnp.where(position < filled[:, None], leading, -1)
    return doc_id.reshape(-1).astype(jnp.int32)


def strengthened(drawn, key, source, target, shards_of, factor):
    def block_of(dim):
        return (jnp.arange(drawn.shape[dim]) // (drawn.shape[dim] // shards_of)).reshape((-1,) + (1,) * (drawn.ndim - 1 - dim))

    first = jax.random.permutation(key, shards_of)[block_of(target)]
    other_side = (block_of(target) + shards_of // 2) % shards_of
    return jnp.where((block_of(source) == first) | (block_of(source) == other_side), factor * drawn, drawn)


def level_of(stream_key, extent, cuts, least, largest):
    level = 1.0
    for dim, blocks in cuts:
        draws = jax.random.uniform(jax.random.fold_in(jax.random.fold_in(stream_key, 6), dim), (blocks,), jnp.float32, least / len(cuts), largest / len(cuts))
        level = level * jnp.repeat(jnp.exp(draws), extent[dim] // blocks).reshape((-1,) + (1,) * (len(extent) - 1 - dim))
    return level


def bell_draw(own_key, extent, deviation, reach, cuts=(), dtype=jnp.bfloat16):
    values = deviation * jax.random.normal(own_key, extent, jnp.float32)
    if cuts:
        values = values * level_of(own_key, extent, cuts, -0.22, 0.18)
    return jnp.clip(values, -reach, reach).astype(dtype)


def gaussian_with(stream_key, dims, spread, limit, shards, heavy, kind=jnp.bfloat16):
    values = spread * jax.random.normal(stream_key, dims, jnp.float32)
    if shards:
        values = values * level_of(stream_key, dims, shards, -0.22, 0.18)
    return jnp.clip(strengthened(values, jax.random.fold_in(stream_key, 3), *heavy), -limit, limit).astype(kind)


def setup_inputs(seed: int = 0) -> dict:
    key_of = jax.random.split(jax.random.key(seed), 13)
    block_input = gaussian_with(key_of[0], (TOKENS, D), 1.0, 6.0, ((0, 16),), (0, 1, 16, 2.0))
    document_ids = draw_document_ids(jax.random.fold_in(key_of[12], 71), 0)
    heads_weight = bell_draw(key_of[2], (LAYERS, 3, D, D), D ** -0.5, 0.1875, ((2, 16), (3, 2)))
    merge_weight = bell_draw(key_of[3], (LAYERS, D, D), (D // 16) ** -0.5, 0.75, ((1, 2), (2, 16)))
    up_weight = bell_draw(key_of[4], (LAYERS, D, FF), D ** -0.5, 0.1875, ((1, 16), (2, 2)))
    down_weight = bell_draw(key_of[5], (LAYERS, FF, D), FF ** -0.5, 0.09375, ((1, 2), (2, 16)))
    query_value_bias = bell_draw(key_of[6], (LAYERS, 2, D), 0.5, 3.0, ((2, 2),), jnp.float32)
    up_bias = bell_draw(key_of[7], (LAYERS, FF), 0.5, 3.0, ((1, 2),), jnp.float32)
    output_bias = bell_draw(key_of[8], (LAYERS, 2, D), 0.5, 3.0, (), jnp.float32)
    norm_gain = jnp.clip(1.0 + 0.1 * jax.random.normal(key_of[9], (LAYERS, 2, D), jnp.float32), 0.5, 1.5)
    norm_shift = bell_draw(key_of[10], (LAYERS, 2, D), 0.5, 3.0, (), jnp.float32)
    cotangent = gaussian_with(key_of[11], (TOKENS, D), 1.0, 6.0, ((0, 16),), (0, 1, 16, 2.0))
    return dict(block_input=block_input, document_ids=document_ids, heads_weight=heads_weight, merge_weight=merge_weight, up_weight=up_weight, down_weight=down_weight, query_value_bias=query_value_bias, up_bias=up_bias, output_bias=output_bias, norm_gain=norm_gain, norm_shift=norm_shift, cotangent=cotangent)


EPS = 1e-12
NEG = -1e+30
ROOT_HALF = 0.7071067811865476
INV_ROOT_TAU = 0.3989422804014327

def as_float(array):
    return array.astype(jnp.float32)

def dot_plain(left, right):
    return jnp.dot(as_float(left), as_float(right), preferred_element_type=jnp.float32)

def dot_left(left, right):
    return lax.dot_general(as_float(left), as_float(right), (((0,), (0,)), ((), ())), preferred_element_type=jnp.float32)

def dot_right(left, right):
    return lax.dot_general(as_float(left), as_float(right), (((1,), (1,)), ((), ())), preferred_element_type=jnp.float32)

def normalize(resid):
    average = lax.optimization_barrier(jnp.mean(resid, axis=-1, keepdims=True))
    centered = resid - average
    inv_scale = lax.rsqrt(lax.optimization_barrier(jnp.mean(centered * centered, axis=-1, keepdims=True)) + EPS)
    return (centered * inv_scale, inv_scale)

def normalize_back(grad_out, normed, inv_scale, gain):
    grad_normed = grad_out * gain
    return inv_scale * (grad_normed - lax.optimization_barrier(jnp.mean(grad_normed, axis=-1, keepdims=True)) - normed * lax.optimization_barrier(jnp.mean(grad_normed * normed, axis=-1, keepdims=True)))

def gelu_value(pre_act):
    return 0.5 * pre_act * (1.0 + lax.erf(pre_act * ROOT_HALF))

def gelu_slope(pre_act):
    return 0.5 * (1.0 + lax.erf(pre_act * ROOT_HALF)) + pre_act * jnp.exp(-0.5 * pre_act * pre_act) * INV_ROOT_TAU

def split_heads(array):
    return array.reshape(array.shape[0], -1, HEAD_DIM)

def masked_scores(queries, key_rows, same_doc):
    scores = jnp.einsum('qhd,khd->hqk', as_float(split_heads(queries)), as_float(split_heads(key_rows)))
    scores = scores * HEAD_DIM ** (-0.5)
    return jnp.where(same_doc[None], scores, NEG)

def attend(queries, key_rows, values, same_doc):
    scores = masked_scores(queries, key_rows, same_doc)
    highest = lax.optimization_barrier(jnp.max(scores, axis=-1, keepdims=True))
    log_total = highest + jnp.log(lax.optimization_barrier(jnp.sum(jnp.exp(scores - highest), axis=-1, keepdims=True)))
    probs = jnp.exp(scores - log_total)
    probs_b = probs.astype(jnp.bfloat16)
    context = jnp.einsum('hqk,khd->qhd', as_float(probs_b), as_float(split_heads(values)))
    return (context.reshape(queries.shape[0], -1).astype(jnp.bfloat16), log_total)

def attend_back(queries, key_rows, values, log_total, grad_context, same_doc):
    rows = queries.shape[0]
    scores = masked_scores(queries, key_rows, same_doc)
    probs = jnp.exp(scores - log_total)
    probs_b = probs.astype(jnp.bfloat16)
    grad_heads = as_float(split_heads(grad_context))
    grad_probs = jnp.einsum('qhd,khd->hqk', grad_heads, as_float(split_heads(values)))
    row_inner = lax.optimization_barrier(jnp.sum(probs * grad_probs, axis=-1, keepdims=True))
    grad_scores = (probs * (grad_probs - row_inner) * HEAD_DIM ** (-0.5)).astype(jnp.bfloat16)
    grad_query = jnp.einsum('hqk,khd->qhd', as_float(grad_scores), as_float(split_heads(key_rows)))
    grad_key = jnp.einsum('hqk,qhd->khd', as_float(grad_scores), as_float(split_heads(queries)))
    grad_value = jnp.einsum('hqk,qhd->khd', as_float(probs_b), grad_heads)
    return (grad_query.reshape(rows, -1), grad_key.reshape(rows, -1), grad_value.reshape(rows, -1))

def layer_forward(hidden, params, same_doc):
    heads_w, merge_w, up_w, down_w, qv_bias, inner_bias, out_bias, gains, shifts = params
    inputs = hidden.astype(jnp.bfloat16)
    queries = (dot_plain(inputs, heads_w[0]) + qv_bias[0]).astype(jnp.bfloat16)
    key_rows = dot_plain(inputs, heads_w[1]).astype(jnp.bfloat16)
    values = (dot_plain(inputs, heads_w[2]) + qv_bias[1]).astype(jnp.bfloat16)
    context, log_total = attend(queries, key_rows, values, same_doc)
    first_sum = hidden + dot_plain(context, merge_w) + out_bias[0]
    normed_one, inv_one = normalize(first_sum)
    middle = normed_one * gains[0] + shifts[0]
    mid_inputs = middle.astype(jnp.bfloat16)
    pre_act = dot_plain(mid_inputs, up_w) + inner_bias
    activ = gelu_value(pre_act).astype(jnp.bfloat16)
    second_sum = middle + dot_plain(activ, down_w) + out_bias[1]
    normed_two, inv_two = normalize(second_sum)
    result = normed_two * gains[1] + shifts[1]
    saved = (inputs, queries, key_rows, values, log_total, context, normed_one, inv_one, mid_inputs, pre_act, activ, normed_two, inv_two)
    return (result, saved)

def layer_backward(grad_out, saved, params, same_doc):
    heads_w, merge_w, up_w, down_w, qv_bias, inner_bias, out_bias, gains, shifts = params
    inputs, queries, key_rows, values, log_total, context, normed_one, inv_one, mid_inputs, pre_act, activ, normed_two, inv_two = saved
    gain_two = lax.optimization_barrier(jnp.sum(grad_out * normed_two, axis=0))
    shift_two = lax.optimization_barrier(jnp.sum(grad_out, axis=0))
    grad_second = normalize_back(grad_out, normed_two, inv_two, gains[1])
    bias_two = lax.optimization_barrier(jnp.sum(grad_second, axis=0))
    second_b = grad_second.astype(jnp.bfloat16)
    grad_down = dot_left(activ, second_b)
    grad_pre = dot_right(second_b, down_w) * gelu_slope(pre_act)
    grad_inner = lax.optimization_barrier(jnp.sum(grad_pre, axis=0))
    pre_b = grad_pre.astype(jnp.bfloat16)
    grad_up = dot_left(mid_inputs, pre_b)
    grad_middle = grad_second + dot_right(pre_b, up_w)
    gain_one = lax.optimization_barrier(jnp.sum(grad_middle * normed_one, axis=0))
    shift_one = lax.optimization_barrier(jnp.sum(grad_middle, axis=0))
    grad_first = normalize_back(grad_middle, normed_one, inv_one, gains[0])
    bias_one = lax.optimization_barrier(jnp.sum(grad_first, axis=0))
    first_b = grad_first.astype(jnp.bfloat16)
    grad_merge = dot_left(context, first_b)
    grad_context = dot_right(first_b, merge_w).astype(jnp.bfloat16)
    grad_query, grad_key, grad_value = attend_back(queries, key_rows, values, log_total, grad_context, same_doc)
    grad_qv = jnp.stack([lax.optimization_barrier(jnp.sum(grad_query, axis=0)), lax.optimization_barrier(jnp.sum(grad_value, axis=0))])
    query_b = grad_query.astype(jnp.bfloat16)
    key_b = grad_key.astype(jnp.bfloat16)
    value_b = grad_value.astype(jnp.bfloat16)
    grad_heads = jnp.stack([dot_left(inputs, query_b), dot_left(inputs, key_b), dot_left(inputs, value_b)])
    grad_hidden = grad_first + (dot_right(query_b, heads_w[0]) + dot_right(key_b, heads_w[1]) + dot_right(value_b, heads_w[2]))
    grads = (grad_heads, grad_merge, grad_up, grad_down, grad_qv, grad_inner, jnp.stack([bias_one, bias_two]), jnp.stack([gain_one, gain_two]), jnp.stack([shift_one, shift_two]))
    return (grad_hidden, grads)

def reference(block_input, document_ids, heads_weight, merge_weight, up_weight, down_weight, query_value_bias, up_bias, output_bias, norm_gain, norm_shift, cotangent):
    blocks = block_input.shape[0] // TOK_DEV
    every = (heads_weight, merge_weight, up_weight, down_weight, query_value_bias, up_bias, output_bias, norm_gain, norm_shift)

    def layer_params(layer_index):
        return tuple((array[layer_index] for array in every))

    def one_block(totals, pieces):
        inputs_block, ids_block, cot_block = pieces
        same_doc = ids_block[:, None] == ids_block[None, :]
        live_rows = (ids_block >= 0).astype(jnp.float32)[:, None]
        hidden = inputs_block.astype(jnp.float32)
        saves = []
        for layer_index in range(LAYERS):
            hidden, saved = layer_forward(hidden, layer_params(layer_index), same_doc)
            saves.append(saved)
        output = hidden.astype(jnp.bfloat16)
        grad_hidden = cot_block.astype(jnp.float32) * live_rows
        collected = [None] * LAYERS
        for layer_index in reversed(range(LAYERS)):
            grad_hidden, layer_grads = layer_backward(grad_hidden, saves[layer_index], layer_params(layer_index), same_doc)
            collected[layer_index] = layer_grads
        stacked = tuple((jnp.stack([part[member] for part in collected]) for member in range(9)))
        totals = tuple((total + piece for total, piece in zip(totals, stacked)))
        return (totals, (output, grad_hidden))
    start = tuple((jnp.zeros(array.shape, jnp.float32) for array in every))
    totals, (outputs, grad_inputs) = lax.scan(one_block, start, (block_input.reshape(blocks, TOK_DEV, D), document_ids.reshape(blocks, TOK_DEV), cotangent.reshape(blocks, TOK_DEV, D)))
    return (outputs.reshape(-1, D), grad_inputs.reshape(-1, D), totals[0], totals[1], totals[2], totals[3], totals[4], totals[5], totals[6], totals[7], totals[8])
```

```python
import jax
import jax.numpy as jnp
from jax import lax
from jax.sharding import PartitionSpec as P

HEAD_DIM = 64
EPS = 1e-12
NEG = -1e30
ROOT_HALF = 0.7071067811865476
INV_ROOT_TAU = 0.3989422804014327


def dot_plain(left, right):
    return jnp.dot(left, right, preferred_element_type=jnp.float32)


def dot_left(left, right):
    return lax.dot_general(
        left, right, (((0,), (0,)), ((), ())), preferred_element_type=jnp.float32
    )


def dot_right(left, right):
    return lax.dot_general(
        left, right, (((1,), (1,)), ((), ())), preferred_element_type=jnp.float32
    )


def normalize(resid):
    average = jnp.mean(resid, axis=-1, keepdims=True)
    centered = resid - average
    inv_scale = lax.rsqrt(jnp.mean(centered * centered, axis=-1, keepdims=True) + EPS)
    return (centered * inv_scale, inv_scale)


def normalize_back(grad_out, normed, inv_scale, gain):
    grad_normed = grad_out * gain
    return inv_scale * (
        grad_normed
        - jnp.mean(grad_normed, axis=-1, keepdims=True)
        - normed * jnp.mean(grad_normed * normed, axis=-1, keepdims=True)
    )


def gelu_value(pre_act):
    return 0.5 * pre_act * (1.0 + lax.erf(pre_act * ROOT_HALF))


def gelu_slope(pre_act):
    return (
        0.5 * (1.0 + lax.erf(pre_act * ROOT_HALF))
        + pre_act * jnp.exp(-0.5 * pre_act * pre_act) * INV_ROOT_TAU
    )


def rounded(value):
    return value.astype(jnp.bfloat16)


class Wires:
    def __init__(self, count):
        self.count = count
        self.bits = count.bit_length() - 1
        self.pair = 1 << (self.bits - 2)
        self.doubling = [1 << (self.bits - 1)] + [1 << b for b in range(self.bits - 3, 1, -1)]

    def dp(self, value, mask):
        return lax.ppermute(value, "dp", [(i, i ^ mask) for i in range(self.count)])

    def tensor(self, value):
        return lax.ppermute(value, "tensor", [(0, 1), (1, 0)])

    def canonical(self, index, width, place):
        slot = index // width
        moved = jnp.where(slot & 1 == 1, self.pair, 0)
        for level, mask in enumerate(self.doubling):
            moved = moved | jnp.where((slot >> (level + 1)) & 1 == 1, mask, 0)
        moved = moved | (slot >> (1 + len(self.doubling)))
        base = place & ~self.pair
        return (base ^ moved) * width + index % width

    def gather(self, keep, send, upper):
        other = self.dp(send, self.pair)
        first = jnp.concatenate(
            [jnp.where(upper, other, keep), jnp.where(upper, keep, other)], axis=0
        )
        chunks = [first]
        for mask in self.doubling:
            chunks = chunks + [self.dp(chunk, mask) for chunk in chunks]
        half = len(chunks) // 2
        side_x = [self.dp(chunk, 1) for chunk in chunks]
        side_y = [self.dp(chunk, 2) for chunk in chunks]
        corner = [self.dp(chunk, 1) for chunk in side_y[:half]]
        corner = corner + [self.dp(chunk, 2) for chunk in side_x[half:]]
        return jnp.concatenate(chunks + side_x + side_y + corner, axis=0)

    def scatter(self, left, right, upper):
        per_side = 1 << len(self.doubling)
        half = per_side // 2
        rows = left.shape[1] // (4 * per_side)

        def piece(side, number):
            start = (side * per_side + number) * rows
            return dot_left(left[:, start : start + rows], right)

        corner = [rounded(piece(3, k)) for k in range(per_side)]
        to_y = [self.dp(chunk, 1) for chunk in corner[:half]]
        to_x = [self.dp(chunk, 2) for chunk in corner[half:]]
        side_x = [piece(1, k) for k in range(per_side)]
        side_y = [piece(2, k) for k in range(per_side)]
        for k in range(half):
            side_y[k] = side_y[k] + to_y[k]
            side_x[half + k] = side_x[half + k] + to_x[k]
        from_x = [self.dp(rounded(chunk), 1) for chunk in side_x]
        from_y = [self.dp(rounded(chunk), 2) for chunk in side_y]
        total = [piece(0, k) + from_x[k] + from_y[k] for k in range(per_side)]
        for mask in reversed(self.doubling):
            keep = len(total) // 2
            arrived = [self.dp(rounded(chunk), mask) for chunk in total[keep:]]
            total = [chunk + extra for chunk, extra in zip(total[:keep], arrived)]
        (mine,) = total
        width = mine.shape[0] // 2
        low, high = mine[:width], mine[width:]
        kept = jnp.where(upper, high, low)
        other = self.dp(rounded(jnp.where(upper, low, high)), self.pair).astype(jnp.float32)
        return jnp.stack([jnp.where(upper, other, kept), jnp.where(upper, kept, other)])

    def group_total(self, partial):
        rows = partial.shape[0] // 2
        core = partial[:rows] + self.tensor(rounded(partial[rows:]))
        core = lax.reduce_precision(core, 8, 7)
        return core + self.dp(rounded(core), self.pair).astype(jnp.float32)

    def both(self, own):
        return jnp.concatenate([own, self.tensor(own)], axis=0)

    def token_total(self, value):
        for level in range(self.bits):
            if 1 << level != self.pair:
                value = value + self.dp(value, 1 << level)
        return value


def split_heads(array, blocks):
    return array.reshape(blocks, array.shape[0] // blocks, -1, HEAD_DIM)


def masked_scores(queries, key_rows, same_doc):
    scores = jnp.einsum(
        "bqhd,bkhd->bhqk",
        split_heads(queries, 2),
        split_heads(key_rows, 2),
        preferred_element_type=jnp.float32,
    )
    scores = scores * HEAD_DIM ** (-0.5)
    return jnp.where(same_doc[:, None], scores, NEG)


def attend(queries, key_rows, values, same_doc):
    scores = masked_scores(queries, key_rows, same_doc)
    highest = jnp.max(scores, axis=-1, keepdims=True)
    log_total = highest + jnp.log(jnp.sum(jnp.exp(scores - highest), axis=-1, keepdims=True))
    probs_b = rounded(jnp.exp(scores - log_total))
    context = jnp.einsum(
        "bhqk,bkhd->bqhd", probs_b, split_heads(values, 2), preferred_element_type=jnp.float32
    )
    return (rounded(context.reshape(queries.shape)), log_total)


def attend_back(queries, key_rows, values, log_total, grad_context, same_doc):
    scores = masked_scores(queries, key_rows, same_doc)
    probs = jnp.exp(scores - log_total)
    probs_b = rounded(probs)
    grad_heads = split_heads(grad_context, 2)
    grad_probs = jnp.einsum(
        "bqhd,bkhd->bhqk", grad_heads, split_heads(values, 2), preferred_element_type=jnp.float32
    )
    row_inner = jnp.sum(probs * grad_probs, axis=-1, keepdims=True)
    grad_scores = rounded(probs * (grad_probs - row_inner) * HEAD_DIM ** (-0.5))
    grad_query = jnp.einsum(
        "bhqk,bkhd->bqhd", grad_scores, split_heads(key_rows, 2), preferred_element_type=jnp.float32
    )
    grad_key = jnp.einsum(
        "bhqk,bqhd->bkhd", grad_scores, split_heads(queries, 2), preferred_element_type=jnp.float32
    )
    grad_value = jnp.einsum(
        "bhqk,bqhd->bkhd", probs_b, grad_heads, preferred_element_type=jnp.float32
    )
    shape = queries.shape
    return (grad_query.reshape(shape), grad_key.reshape(shape), grad_value.reshape(shape))


def layer_forward(wires, hidden, inputs, matrices, small, same_doc):
    heads_w, up_w, down_w = matrices
    qv_bias, inner_bias, out_bias, gains, shifts = small
    quarter = heads_w.shape[1] // 4
    projected = dot_plain(inputs, heads_w[:, : 3 * quarter])
    queries = rounded(projected[:, :quarter] + qv_bias[0])
    key_rows = rounded(projected[:, quarter : 2 * quarter])
    values = rounded(projected[:, 2 * quarter :] + qv_bias[1])
    context, log_total = attend(queries, key_rows, values, same_doc)
    merged = dot_right(context, heads_w[:, 3 * quarter :])
    first_sum = hidden + (wires.group_total(merged) + out_bias[0])
    normed_one, inv_one = normalize(first_sum)
    middle = normed_one * gains[0] + shifts[0]
    mid_inputs = wires.both(rounded(middle))
    pre_act = dot_plain(mid_inputs, up_w) + inner_bias
    activ = rounded(gelu_value(pre_act))
    second_sum = middle + (wires.group_total(dot_right(activ, down_w)) + out_bias[1])
    normed_two, inv_two = normalize(second_sum)
    result = normed_two * gains[1] + shifts[1]
    saved = (
        inputs,
        queries,
        key_rows,
        values,
        log_total,
        context,
        normed_one,
        inv_one,
        mid_inputs,
        pre_act,
        activ,
        normed_two,
        inv_two,
    )
    return (result, saved)


def layer_backward(wires, grad_out, saved, matrices, small, same_doc, upper):
    heads_w, up_w, down_w = matrices
    qv_bias, inner_bias, out_bias, gains, shifts = small
    (
        inputs,
        queries,
        key_rows,
        values,
        log_total,
        context,
        normed_one,
        inv_one,
        mid_inputs,
        pre_act,
        activ,
        normed_two,
        inv_two,
    ) = saved
    quarter = heads_w.shape[1] // 4
    gain_two = jnp.sum(grad_out * normed_two, axis=0)
    shift_two = jnp.sum(grad_out, axis=0)
    grad_second = normalize_back(grad_out, normed_two, inv_two, gains[1])
    bias_two = jnp.sum(grad_second, axis=0)
    second_b = wires.both(rounded(grad_second))
    grad_pre = dot_plain(second_b, down_w) * gelu_slope(pre_act)
    grad_inner = jnp.sum(grad_pre, axis=0)
    pre_b = rounded(grad_pre)
    through_up = dot_right(pre_b, up_w)
    grad_down = wires.scatter(second_b, activ, upper)
    grad_middle = grad_second + wires.group_total(through_up)
    grad_up = wires.scatter(mid_inputs, pre_b, upper)
    gain_one = jnp.sum(grad_middle * normed_one, axis=0)
    shift_one = jnp.sum(grad_middle, axis=0)
    grad_first = normalize_back(grad_middle, normed_one, inv_one, gains[0])
    bias_one = jnp.sum(grad_first, axis=0)
    first_b = wires.both(rounded(grad_first))
    grad_context = rounded(dot_plain(first_b, heads_w[:, 3 * quarter :]))
    grad_query, grad_key, grad_value = attend_back(
        queries, key_rows, values, log_total, grad_context, same_doc
    )
    grad_qv = jnp.stack([jnp.sum(grad_query, axis=0), jnp.sum(grad_value, axis=0)])
    heads_b = jnp.concatenate([rounded(grad_query), rounded(grad_key), rounded(grad_value)], axis=1)
    through_heads = dot_right(heads_b, heads_w[:, : 3 * quarter])
    grad_hidden = grad_first + wires.group_total(through_heads)
    grad_merge = wires.scatter(first_b, context, upper)
    grad_heads = wires.scatter(inputs, heads_b, upper)
    large = (grad_heads, grad_merge, grad_up, grad_down)
    by_feature = jnp.stack([bias_one, bias_two, gain_one, gain_two, shift_one, shift_two])
    return (grad_hidden, large, (by_feature, grad_qv, grad_inner))


def shards(
    wires,
    block_input,
    document_ids,
    heads_weight,
    merge_weight,
    up_weight,
    down_weight,
    query_value_bias,
    up_bias,
    output_bias,
    norm_gain,
    norm_shift,
    cotangent,
):
    depth = heads_weight.shape[0]
    model = block_input.shape[1]
    place = lax.axis_index("dp")
    upper_bit = (place // wires.pair) % 2
    upper = upper_bit == 1
    at_home = upper_bit == lax.axis_index("tensor")
    width = heads_weight.shape[2]
    quarter = heads_weight.shape[3] // 2
    inner = up_weight.shape[2] // 2

    def parts(array, axis):
        size = array.shape[axis] // 2
        low = lax.slice_in_dim(array, 0, size, axis=axis)
        high = lax.slice_in_dim(array, size, 2 * size, axis=axis)
        return jnp.where(upper, high, low), jnp.where(upper, low, high)

    def fetch(layer_index):
        heads_keep, heads_send = parts(heads_weight[layer_index], 2)
        merge_keep, merge_send = parts(merge_weight[layer_index], 0)

        def unit(heads_part, merge_part):
            return jnp.concatenate([heads_part[0], heads_part[1], heads_part[2], merge_part.T], axis=1)

        up_keep, up_send = parts(up_weight[layer_index], 1)
        down_keep, down_send = parts(down_weight[layer_index], 0)
        return (
            wires.gather(unit(heads_keep, merge_keep), unit(heads_send, merge_send), upper),
            wires.gather(up_keep, up_send, upper),
            wires.gather(down_keep.T, down_send.T, upper),
        )

    rows = lax.broadcasted_iota(jnp.int32, (model, model), 0)
    columns = lax.broadcasted_iota(jnp.int32, (model, model), 1)
    to_own = rows == wires.canonical(columns, width, place)
    exact = lax.Precision.HIGHEST

    def own_order(array):
        if array.dtype == jnp.bfloat16:
            return rounded(dot_plain(array, to_own.astype(jnp.bfloat16)))
        return jnp.dot(array, to_own.astype(jnp.float32), precision=exact)

    def plain_order(array):
        if array.dtype == jnp.bfloat16:
            return rounded(dot_right(array, to_own.astype(jnp.bfloat16)))
        return lax.dot_general(
            array, to_own.astype(jnp.float32), (((1,), (1,)), ((), ())), precision=exact
        )

    def blocks(array):
        other = wires.dp(array, wires.pair)
        return jnp.where(at_home, array, other), jnp.where(at_home, other, array)

    by_feature = own_order(
        jnp.concatenate([output_bias, norm_gain, norm_shift], axis=1).reshape(-1, model)
    ).reshape(depth, 3, 2, model)
    qv_bias = parts(query_value_bias, 2)[0]
    inner_bias = parts(up_bias, 1)[0]

    def small_params(layer_index):
        return (
            qv_bias[layer_index],
            inner_bias[layer_index],
            by_feature[layer_index, 0],
            by_feature[layer_index, 1],
            by_feature[layer_index, 2],
        )

    ids_own, ids_other = blocks(document_ids)
    ids = jnp.stack([ids_own, ids_other])
    same_doc = ids[:, :, None] == ids[:, None, :]
    live_rows = (ids_own >= 0).astype(jnp.float32)[:, None]
    input_own, input_other = blocks(own_order(block_input))

    kept = [fetch(layer_index) for layer_index in range(depth)]
    saves = []
    inputs = jnp.concatenate([input_own, input_other], axis=0)
    hidden = input_own.astype(jnp.float32)
    for layer_index in range(depth):
        if layer_index > 0:
            inputs = wires.both(rounded(hidden))
        hidden, saved = layer_forward(
            wires, hidden, inputs, kept[layer_index], small_params(layer_index), same_doc
        )
        saves.append(saved)
    output_own = rounded(hidden)
    block_output = plain_order(jnp.where(at_home, output_own, wires.tensor(output_own)))

    grad_hidden = blocks(own_order(cotangent))[0].astype(jnp.float32) * live_rows
    large_parts = [None] * depth
    small_parts = [None] * depth
    for layer_index in reversed(range(depth)):
        grad_hidden, large_parts[layer_index], small_parts[layer_index] = layer_backward(
            wires,
            grad_hidden,
            saves[layer_index],
            kept[layer_index],
            small_params(layer_index),
            same_doc,
            upper,
        )
    grad_input = plain_order(jnp.where(at_home, grad_hidden, wires.tensor(grad_hidden)))

    def columns_of(part):
        return jnp.concatenate([part[0], part[1]], axis=1)

    grad_heads = jnp.stack(
        [
            jnp.stack(
                [
                    columns_of(large[0][:, :, k * quarter : (k + 1) * quarter])
                    for k in range(3)
                ]
            )
            for large in large_parts
        ]
    )
    grad_merge = jnp.stack([columns_of(large[1]).T for large in large_parts])
    grad_up = jnp.stack([columns_of(large[2]) for large in large_parts])
    grad_down = jnp.stack([columns_of(large[3]).T for large in large_parts])

    feature_sums = plain_order(jnp.concatenate([part[0] for part in small_parts], axis=0))
    feature_sums = feature_sums + wires.tensor(feature_sums)
    head_sums = jnp.concatenate(
        [jnp.concatenate([part[1].reshape(-1), part[2]]) for part in small_parts]
    ).reshape(1, -1)
    summed = wires.token_total(jnp.concatenate([feature_sums.reshape(1, -1), head_sums], axis=1))[0]
    feature_sums = summed[: 6 * depth * model].reshape(depth, 3, 2, model)
    head_sums = summed[6 * depth * model :].reshape(depth, -1)
    other = wires.dp(head_sums, wires.pair)
    low, high = jnp.where(upper, other, head_sums), jnp.where(upper, head_sums, other)
    qv = [array[:, : 2 * quarter].reshape(depth, 2, quarter) for array in (low, high)]
    grad_qv = jnp.concatenate(qv, axis=2)
    grad_inner = jnp.concatenate([low[:, 2 * quarter :], high[:, 2 * quarter :]], axis=1)
    return (
        block_output,
        grad_input,
        grad_heads,
        grad_merge,
        grad_up,
        grad_down,
        grad_qv,
        grad_inner,
        feature_sums[:, 0],
        feature_sums[:, 1],
        feature_sums[:, 2],
    )


def solution(mesh):
    wires = Wires(mesh.shape["dp"])

    def body(*arrays):
        return shards(wires, *arrays)

    return jax.shard_map(
        body,
        mesh=mesh,
        in_specs=(
            P("dp", None),
            P("dp"),
            P(None, None, "dp", "tensor"),
            P(None, "tensor", "dp"),
            P(None, "dp", "tensor"),
            P(None, "tensor", "dp"),
            P(None, None, "tensor"),
            P(None, "tensor"),
            P(),
            P(),
            P(),
            P("dp", None),
        ),
        out_specs=(
            P("dp", None),
            P("dp", None),
            P(None, None, "dp", "tensor"),
            P(None, "tensor", "dp"),
            P(None, "dp", "tensor"),
            P(None, "tensor", "dp"),
            P(None, None, "tensor"),
            P(None, "tensor"),
            P(),
            P(),
            P(),
        ),
        check_vma=False,
    )
```
